32 devices in a mesh: groups: 2 (over x), rows: 16 (over z, y, core).
Axes of the slice: x: 2, y: 2, z: 4, core: 2. Of those that a mesh axis runs over, the one named last changes fastest.
Arguments:
- coeffs: bfloat16 [1536, 8192], P(('groups', 'rows')), parts along dimension 0, may hold values from -0.0625 to 0.0625
- ham_blocks: bfloat16 [256, 16, 64, 64], P(('groups', 'rows')), parts along dimension 0, may hold values from -0.1875 to 0.1875
- metric_blocks: bfloat16 [256, 16, 64, 64], P(('groups', 'rows')), parts along dimension 0, may hold values from -0.0625 to 0.0625
- block_cols: int32 [256, 16], P(('groups', 'rows')), parts along dimension 0, may hold values from 0 to 127, as said below
- block_counts: int32 [256], P(('groups', 'rows')), parts along dimension 0, may hold values from 4 to 16, as said below
Outputs:
- gradient: bfloat16 [1536, 8192], P(('groups', 'rows')), parts along dimension 0
- band_hamiltonian: float32 [1536, 768], P('groups'), parts along dimension 0
- energy: float32 [2], P('groups'), parts along dimension 0
The draws below stay inside these ranges and needn't reach their ends.
There are 2 independent parts, one for each index of `groups`. The reference program is written for one: setup_inputs(seed, part) draws one part's arguments, and reference() takes and returns one part's arrays. A program takes and returns all parts, laid end to end along the dimension named above; each array names one. Nothing has to cross between parts.
Inputs may be any that keep to these rules, and one draw needn't show every extreme that they name: `block_cols`: slot 0 of block row b holds b itself; every entry lies within 8 block rows of its own row. `block_counts`: slots of a row at or past its count are padding and their blocks are ignored; some row uses all 16 slots.
All inputs are finite; a program needn't handle non-finite values.
Results may differ from the reference program's by a relative error of at most 0.0078.
Values may be sent and summed in bfloat16 or wider, within the bound.
No kernel may reach another device: no remote copies, remote signals or barrier semaphores. Data moves between devices by JAX's collectives and lax.ppermute only.
A program may use at most 64 MiB of HBM per device.

```python
import math
import jax
import jax.numpy as jnp
from jax import lax

M = 768
BLK = 64
NB = 16
BR_DEV = 8
NBR = 128
NORB = 8192


def draw_block_cols(key, part):
    own_row = jnp.arange(NBR, dtype=jnp.int32)[:, None]
    offsets = jax.random.randint(key, (NBR, NB), -BR_DEV, BR_DEV + 1, dtype=jnp.int32)
    slot_index = jnp.arange(NB, dtype=jnp.int32)[None, :]
    offsets = jnp.where(slot_index == 0, 0, offsets)
    return jnp.clip(own_row + offsets, 0, NBR - 1).astype(jnp.int32)


def draw_block_counts(key, part):
    lowest = max(1, NB // 4)
    counts = jax.random.randint(key, (NBR,), lowest, NB + 1, dtype=jnp.int32)
    chosen = jax.random.randint(jax.random.fold_in(key, 1), (), 0, NBR, dtype=jnp.int32)
    second = (chosen + NBR // 2) % NBR
    row_index = jnp.arange(NBR, dtype=jnp.int32)
    counts = jnp.where(row_index == chosen, NB, counts)
    counts = jnp.where(row_index == second, lowest, counts)
    return counts.astype(jnp.int32)


def block_levels(stream_key, shape, shards, low, largest):
    gain, own = 1.0, jax.random.fold_in(stream_key, 6)
    for dim, blocks in shards:
        heights = jnp.exp(jax.random.uniform(jax.random.fold_in(own, dim), (blocks,), jnp.float32, low / len(shards), largest / len(shards)))
        gain = gain * jnp.repeat(heights, shape[dim] // blocks).reshape([-1 if axis == dim else 1 for axis in range(len(shape))])
    return gain


def centred(rng, shape, deviation, bound, pieces=(), kind=jnp.bfloat16):
    drawn = deviation * jax.random.normal(rng, shape, jnp.float32)
    if pieces:
        drawn = drawn * block_levels(rng, shape, pieces, -0.22, 0.18)
    return jnp.clip(drawn, -bound, bound).astype(kind)


def setup_inputs(seed: int = 0, part: int = 0) -> dict:
    seeds = jax.random.split(jax.random.key(seed), 6)
    own_keys = jax.random.split(jax.random.fold_in(seeds[5], part), 6)
    coeffs = centred(own_keys[0], (M, NORB), NORB ** -0.5, 0.0625, ((0, 16),))
    ham_blocks = centred(own_keys[1], (NBR, NB, BLK, BLK), (NB * BLK) ** -0.5, 0.1875, ((0, 16),))
    metric_blocks = centred(own_keys[2], (NBR, NB, BLK, BLK), (8 * NB * BLK) ** -0.5, 0.0625, ((0, 16),))
    block_cols = draw_block_cols(jax.random.fold_in(jax.random.fold_in(seeds[5], part), 71), part)
    block_counts = draw_block_counts(jax.random.fold_in(jax.random.fold_in(seeds[5], part), 71), part)
    return dict(coeffs=coeffs, ham_blocks=ham_blocks, metric_blocks=metric_blocks, block_cols=block_cols, block_counts=block_counts)


def reference(coeffs, ham_blocks, metric_blocks, block_cols, block_counts):
    band_total, orbitals = coeffs.shape
    block_total, slot_count, blocksz, _ = ham_blocks.shape
    stacked = coeffs.reshape(band_total, block_total, blocksz)
    row_mask = (jnp.arange(slot_count, dtype=jnp.int32)[None, :] < block_counts[:, None]).astype(jnp.float32)[:, :, None, None]
    span_rows = 8

    def apply_group(step_index):
        offset = step_index * span_rows
        cols_group = lax.dynamic_slice_in_dim(block_cols, offset, span_rows, 0)
        mask_group = lax.dynamic_slice_in_dim(row_mask, offset, span_rows, 0)
        ham_group = lax.dynamic_slice_in_dim(ham_blocks, offset, span_rows, 0).astype(jnp.float32) * mask_group
        metric_group = lax.dynamic_slice_in_dim(metric_blocks, offset, span_rows, 0).astype(jnp.float32) * mask_group
        picked = jnp.take(stacked, cols_group, axis=1).astype(jnp.float32)
        ham_out = jnp.einsum('jkrc,mjkc->mjr', ham_group, picked, precision=lax.Precision.HIGHEST)
        metric_out = jnp.einsum('jkrc,mjkc->mjr', metric_group, picked, precision=lax.Precision.HIGHEST)
        return (ham_out, metric_out)
    ham_parts, metric_parts = lax.map(apply_group, jnp.arange(block_total // span_rows, dtype=jnp.int32))
    ham_full = jnp.transpose(ham_parts, (1, 0, 2, 3)).reshape(band_total, orbitals)
    metric_full = jnp.transpose(metric_parts, (1, 0, 2, 3)).reshape(band_total, orbitals)
    ham_prod = ham_full.astype(jnp.bfloat16)
    metric_prod = (coeffs.astype(jnp.float32) + metric_full).astype(jnp.bfloat16)
    ham_gram = jnp.dot(ham_prod, coeffs.T, preferred_element_type=jnp.float32)
    metric_gram = jnp.dot(metric_prod, coeffs.T, preferred_element_type=jnp.float32)
    ham_band = ham_gram.astype(jnp.bfloat16)
    metric_band = metric_gram.astype(jnp.bfloat16)
    factor = math.sqrt(NORB)
    ham_wide = ham_band.astype(jnp.float32)
    metric_wide = metric_band.astype(jnp.float32)
    band_hamiltonian = factor * ham_wide
    energy = factor * (2.0 * jnp.trace(ham_wide) - jnp.sum(metric_wide * ham_wide.T))
    grad_full = 4.0 * ham_prod.astype(jnp.float32) - 2.0 * jnp.dot(ham_band, metric_prod, preferred_element_type=jnp.float32) - 2.0 * jnp.dot(metric_band, ham_prod, preferred_element_type=jnp.float32)
    gradient = (factor * grad_full).astype(jnp.bfloat16)
    return (gradient, band_hamiltonian, energy.reshape(1))
```

```python
import functools
import math

import jax
import jax.numpy as jnp
from jax import lax
from jax.experimental import pallas as pl
from jax.experimental.pallas import tpu as pltpu
from jax.sharding import PartitionSpec as P

NT = (((1,), (1,)), ((), ()))


def nt_dot(left, right):
    return lax.dot_general(left, right, NT, preferred_element_type=jnp.float32)


def expand_kernel(cols_ref, counts_ref, ham_ref, metric_ref, wide_ref, acc_ref):
    row = pl.program_id(0)
    slots, size = ham_ref.shape[1], ham_ref.shape[2]
    acc_ref[...] = jnp.zeros_like(acc_ref)
    half = lax.broadcasted_iota(jnp.int32, (size, 2 * size), 1) // size
    for slot in range(slots):
        col = cols_ref[row, slot]
        want = jnp.where(slot < counts_ref[row], col % 2, 2)
        keep = half == want
        lanes = pl.ds(pl.multiple_of((col // 2) * 2 * size, 2 * size), 2 * size)
        for which, blocks in enumerate((ham_ref, metric_ref)):
            block = blocks[0, slot].astype(jnp.float32)
            twice = jnp.concatenate([block, block], axis=1)
            acc_ref[which, :, lanes] += jnp.where(keep, twice, 0.0)
    wide_ref[...] = acc_ref[...].astype(wide_ref.dtype)


def expand(cols, counts, ham_blocks, metric_blocks):
    rows, slots, size, _ = ham_blocks.shape
    width = 3 * rows * size
    blocks_spec = pl.BlockSpec((1, slots, size, size), lambda b, *_: (b, 0, 0, 0))
    return pl.pallas_call(
        expand_kernel,
        out_shape=jax.ShapeDtypeStruct((2, rows * size, width), jnp.bfloat16),
        grid_spec=pltpu.PrefetchScalarGridSpec(
            num_scalar_prefetch=2,
            grid=(rows,),
            in_specs=[blocks_spec, blocks_spec],
            out_specs=pl.BlockSpec((2, size, width), lambda b, *_: (0, b, 0)),
            scratch_shapes=[pltpu.VMEM((2, size, width), jnp.float32)],
        ),
        compiler_params=pltpu.CompilerParams(vmem_limit_bytes=16 * 2**20),
        cost_estimate=pl.CostEstimate(
            flops=2 * ham_blocks.size, bytes_accessed=16 * 2**20, transcendentals=0
        ),
        name="expand",
    )(cols, counts, ham_blocks, metric_blocks)


def product_kernel(left_ref, own_ref, right_ref, all_ref, wide_ref, ham_ref, metric_ref, ham_gram_ref, metric_gram_ref):
    span = own_ref.shape[1]
    own = own_ref[...]

    def apply(which):
        total = nt_dot(own, wide_ref[which, :, span : 2 * span])
        total += nt_dot(left_ref[...], wide_ref[which, :, :span])
        return total + nt_dot(right_ref[...], wide_ref[which, :, 2 * span :])

    ham = apply(0).astype(jnp.bfloat16)
    metric = (own.astype(jnp.float32) + apply(1)).astype(jnp.bfloat16)
    ham_ref[...] = ham
    metric_ref[...] = metric
    ham_gram_ref[...] = nt_dot(ham, all_ref[...])
    metric_gram_ref[...] = nt_dot(metric, all_ref[...])


def product(left, own, right, wide, steps=2):
    bands, span = own.shape
    rows = bands // steps
    part = pl.BlockSpec((rows, span), lambda i, *_: (i, 0))
    square = pl.BlockSpec((rows, bands), lambda i, *_: (i, 0))
    return pl.pallas_call(
        product_kernel,
        out_shape=(
            jax.ShapeDtypeStruct((bands, span), jnp.bfloat16),
            jax.ShapeDtypeStruct((bands, span), jnp.bfloat16),
            jax.ShapeDtypeStruct((bands, bands), jnp.float32),
            jax.ShapeDtypeStruct((bands, bands), jnp.float32),
        ),
        grid_spec=pl.GridSpec(
            grid=(steps,),
            in_specs=[
                part,
                part,
                part,
                pl.BlockSpec((bands, span), lambda i, *_: (0, 0)),
                pl.BlockSpec(wide.shape, lambda i, *_: (0, 0, 0)),
            ],
            out_specs=[part, part, square, square],
        ),
        compiler_params=pltpu.CompilerParams(vmem_limit_bytes=32 * 2**20),
        cost_estimate=pl.CostEstimate(
            flops=2 * bands * span * (6 * span + 2 * bands), bytes_accessed=13 * 2**20, transcendentals=0
        ),
        name="product",
    )(left, own, right, own, wide)


def gradient_kernel(factor, ham_band_ref, metric_band_ref, part_ref, ham_ref, metric_ref, out_ref):
    total = jnp.dot(ham_band_ref[...], metric_ref[...], preferred_element_type=jnp.float32)
    total += jnp.dot(metric_band_ref[...], ham_ref[...], preferred_element_type=jnp.float32)
    out_ref[...] = (factor * (4.0 * part_ref[...].astype(jnp.float32) - 2.0 * total)).astype(jnp.bfloat16)


def gradient_of(factor, ham_band, metric_band, ham_prod, metric_prod, steps=2):
    bands, span = ham_prod.shape
    rows = bands // steps
    square = pl.BlockSpec((rows, bands), lambda i, *_: (i, 0))
    part = pl.BlockSpec((rows, span), lambda i, *_: (i, 0))
    whole = pl.BlockSpec((bands, span), lambda i, *_: (0, 0))
    return pl.pallas_call(
        functools.partial(gradient_kernel, factor),
        out_shape=jax.ShapeDtypeStruct((bands, span), jnp.bfloat16),
        grid_spec=pl.GridSpec(
            grid=(steps,),
            in_specs=[square, square, part, whole, whole],
            out_specs=part,
        ),
        compiler_params=pltpu.CompilerParams(vmem_limit_bytes=24 * 2**20),
        cost_estimate=pl.CostEstimate(
            flops=4 * bands * bands * span, bytes_accessed=6 * 2**20, transcendentals=0
        ),
        name="gradient",
    )(ham_band, metric_band, ham_prod, ham_prod, metric_prod)


def swap(value, bit):
    count = lax.axis_size("rows")
    return lax.ppermute(value, "rows", [(i, i ^ bit) for i in range(count)])


def fill_row(cols, blocks_of, acc_ref, size):
    half = lax.broadcasted_iota(jnp.int32, (size, 2 * size), 1) // size
    for slot, col in enumerate(cols):
        want = jnp.where(col < 0, 2, col % 2)
        lanes = at_block(jnp.maximum(col, 0) // 2, 2 * size)
        for which, block in enumerate(blocks_of(slot)):
            block = block.astype(jnp.float32)
            twice = jnp.concatenate([block, block], axis=1)
            acc_ref[which, :, lanes] += jnp.where(half == want, twice, 0.0)


def write_levels(acc_ref, inner_ref, outer_ref):
    total = acc_ref[...]
    high = total.astype(jnp.bfloat16)
    low = (total - high.astype(jnp.float32)).astype(jnp.bfloat16)
    width = inner_ref.shape[-1]
    for level, value in enumerate((high, low)):
        inner_ref[level] = value[:, :, :width]
        outer_ref[level] = value[:, :, width:]


def expand_own_kernel(cols_ref, ham_ref, metric_ref, inner_ref, outer_ref, packed_ref, acc_ref):
    row = pl.program_id(0)
    slots, size = ham_ref.shape[1], ham_ref.shape[2]
    acc_ref[...] = jnp.zeros_like(acc_ref)
    cols = [cols_ref[row, slot] for slot in range(slots)]
    fill_row(cols, lambda slot: (ham_ref[0, slot], metric_ref[0, slot]), acc_ref, size)
    write_levels(acc_ref, inner_ref, outer_ref)
    for which, blocks_ref in enumerate((ham_ref, metric_ref)):
        for slot in range(slots // 2):
            both = jnp.concatenate([blocks_ref[0, slot], blocks_ref[0, slot + slots // 2]], axis=1)
            packed_ref[which, 0, slot] = both


def expand_packed_kernel(cols_ref, packed_ref, inner_ref, outer_ref, acc_ref):
    row = pl.program_id(0)
    pairs, size = packed_ref.shape[2], packed_ref.shape[3]
    acc_ref[...] = jnp.zeros_like(acc_ref)

    def blocks_of(slot):
        lanes = slice(0, size) if slot < pairs else slice(size, 2 * size)
        return [packed_ref[which, 0, slot % pairs][:, lanes] for which in range(2)]

    fill_row([cols_ref[row, slot] for slot in range(2 * pairs)], blocks_of, acc_ref, size)
    write_levels(acc_ref, inner_ref, outer_ref)


def expand_call(cols, *blocks):
    rows, slots = cols.shape
    size = blocks[0].shape[3]
    span = rows * size
    packed = jax.ShapeDtypeStruct((2, rows, slots // 2, size, 2 * size), jnp.bfloat16)
    packed_spec = pl.BlockSpec((2, 1, slots // 2, size, 2 * size), lambda b, *_: (0, b, 0, 0, 0))
    blocks_spec = pl.BlockSpec((1, slots, size, size), lambda b, *_: (b, 0, 0, 0))
    own = len(blocks) == 2
    return pl.pallas_call(
        expand_own_kernel if own else expand_packed_kernel,
        out_shape=[
            jax.ShapeDtypeStruct((2, 2, span, 2 * span), jnp.bfloat16),
            jax.ShapeDtypeStruct((2, 2, span, span), jnp.bfloat16),
        ]
        + [packed] * own,
        grid_spec=pltpu.PrefetchScalarGridSpec(
            num_scalar_prefetch=1,
            grid=(rows,),
            in_specs=[blocks_spec, blocks_spec] if own else [packed_spec],
            out_specs=[
                pl.BlockSpec((2, 2, size, 2 * span), lambda b, *_: (0, 0, b, 0)),
                pl.BlockSpec((2, 2, size, span), lambda b, *_: (0, 0, b, 0)),
            ]
            + [packed_spec] * own,
            scratch_shapes=[pltpu.VMEM((2, size, 3 * span), jnp.float32)],
        ),
        compiler_params=pltpu.CompilerParams(vmem_limit_bytes=16 * 2**20),
        cost_estimate=pl.CostEstimate(flops=0, bytes_accessed=1024, transcendentals=0),
        name="expand_own" if own else "expand_packed",
    )(cols, *blocks)


def tie(value, *before):
    return lax.optimization_barrier((value, *before))[0]


def at_block(block, piece):
    return pl.ds(pl.multiple_of(block * piece, piece), piece)


def whole_call(kernel, name, outs, scratch=(), limit=8):
    vmem, smem = pl.BlockSpec(memory_space=pltpu.VMEM), pl.BlockSpec(memory_space=pltpu.SMEM)

    def call(scalars, *args):
        return pl.pallas_call(
            kernel,
            out_shape=tuple(jax.ShapeDtypeStruct(shape, dtype) for shape, dtype in outs),
            in_specs=[smem] + [vmem] * len(args),
            out_specs=tuple(smem if shape == (1, 1) else vmem for shape, _ in outs),
            scratch_shapes=scratch,
            compiler_params=pltpu.CompilerParams(vmem_limit_bytes=limit * 2**20),
            cost_estimate=pl.CostEstimate(flops=0, bytes_accessed=1024, transcendentals=0),
            name=name,
        )(scalars, *args)

    return call


def split_kernel(place_ref, coeffs_ref, *out_refs):
    width = out_refs[0].shape[1]
    for step, out_ref in enumerate(out_refs):
        out_ref[...] = coeffs_ref[:, at_block(place_ref[0] ^ step, width)]


def join_kernel(place_ref, *refs):
    *part_refs, out_ref = refs
    width = part_refs[0].shape[1]
    for step, part_ref in enumerate(part_refs):
        out_ref[:, at_block(place_ref[0] ^ step, width)] = part_ref[...]


def stack_kernel(place_ref, *refs):
    *part_refs, out_ref, low_ref, high_ref = refs
    piece, width = part_refs[0].shape
    for step, part_ref in enumerate(part_refs):
        rows = at_block(place_ref[0] ^ step, piece)
        part = part_ref[...]
        out_ref[rows, :] = part
        low_ref[rows, :] = part[:, : width // 2]
        high_ref[rows, :] = part[:, width // 2 :]


def inner_kernel(piece, place_ref, own_ref, cross_ref, mine_ref, other_ref, all_ref, sums_ref):
    core = place_ref[1]
    rows, width = own_ref.shape
    span = width // 2
    for chip in range(rows // piece):
        source = pl.ds(chip * piece, piece)
        all_ref[at_block(2 * chip + core, piece), :] = own_ref[source, :]
        all_ref[at_block(2 * chip + 1 - core, piece), :] = cross_ref[source, :]
    own = own_ref[...]
    for turn, wide_ref in enumerate((mine_ref, other_ref)):
        at = core if turn == 0 else 1 - core
        for which in range(2):
            total = nt_dot(own, wide_ref[1, which]) + nt_dot(own, wide_ref[0, which])
            if which == 1:
                total += own_ref[:, at_block(at, span)].astype(jnp.float32)
            sums_ref[turn, which] = total


def outer_kernel(
    place_ref, sums_ref, all_ref, left_ref, right_ref, mine_ref, other_ref,
    prods_ref, keep_h_ref, send_h_ref, keep_m_ref, *refs,
):
    *send_m_refs, trace_ref, gram_ref = refs
    core, side, line = place_ref[1], place_ref[2], place_ref[3]
    rows, span = left_ref.shape
    lines, piece = keep_h_ref.shape[:2]
    first = core == 0
    left, right = left_ref[...], right_ref[...]
    grams = [None, None]
    for turn, wide_ref in enumerate((mine_ref, other_ref)):
        at = core if turn == 0 else 1 - core
        outer = jnp.where(first, left, right) if turn == 0 else jnp.where(first, right, left)
        columns = at_block(at, span)
        for which in range(2):
            total = sums_ref[turn, which] + nt_dot(outer, wide_ref[1, which]) + nt_dot(outer, wide_ref[0, which])
            prod = total.astype(jnp.bfloat16)
            prods_ref[which, :, columns] = prod
            part = nt_dot(prod, all_ref[:, columns])
            grams[which] = part if grams[which] is None else grams[which] + part
    row = lax.broadcasted_iota(jnp.int32, (rows, 2 * rows), 0)
    col = lax.broadcasted_iota(jnp.int32, (rows, 2 * rows), 1)
    hit = col == row + (row // piece + core) * piece
    trace_ref[...] = jnp.zeros_like(trace_ref)
    for which in range(2):
        trace_ref[which : which + 1, :] = jnp.sum(jnp.where(hit, grams[which], 0.0), axis=0, keepdims=True)
        gram_ref[which] = grams[which]
    for at in range(lines):
        keep_h_ref[at] = gram_ref[0, at_block(2 * at + side, piece), :]
        send_h_ref[at] = gram_ref[0, at_block(2 * at + 1 - side, piece), :].astype(jnp.bfloat16)
    keep_m_ref[...] = gram_ref[1, at_block(line, 2 * piece), :]
    for step, send_ref in enumerate(send_m_refs, 1):
        send_ref[...] = gram_ref[1, at_block(line ^ step, 2 * piece), :].astype(jnp.bfloat16)


def sum_side_kernel(place_ref, keep_ref, got_ref, trace_ref, got_trace_ref, next_ref, next_trace_ref, *send_refs):
    line = place_ref[3]
    next_ref[...] = keep_ref[line] + got_ref[line].astype(jnp.float32)
    for step, send_ref in enumerate(send_refs, 1):
        at = line ^ step
        send_ref[...] = (keep_ref[at] + got_ref[at].astype(jnp.float32)).astype(jnp.bfloat16)
    next_trace_ref[...] = trace_ref[...] + got_trace_ref[...]


def sum_lines_kernel(place_ref, keep_ref, *refs):
    *got_refs, next_ref, send_ref, total_ref = refs
    side = place_ref[2]
    total = keep_ref[...]
    for got_ref in got_refs:
        total += got_ref[...].astype(jnp.float32)
    total_ref[...] = total
    piece = next_ref.shape[0]
    next_ref[...] = total_ref[at_block(side, piece), :]
    send_ref[...] = total_ref[at_block(1 - side, piece), :].astype(jnp.bfloat16)


def last_ham_kernel(place_ref, keep_ref, trace_ref, got_trace_ref, *refs):
    *got_refs, out_ref, next_trace_ref = refs
    total = keep_ref[...]
    for got_ref in got_refs:
        total += got_ref[...].astype(jnp.float32)
    out_ref[...] = total.astype(jnp.bfloat16)
    next_trace_ref[...] = trace_ref[...] + got_trace_ref[...]


def last_metric_kernel(place_ref, keep_ref, got_ref, out_ref):
    out_ref[...] = (keep_ref[...] + got_ref[...].astype(jnp.float32)).astype(jnp.bfloat16)


def interleave(all_ref, mine_ref, cross_ref, core, piece):
    for chip in range(mine_ref.shape[1] // piece):
        source = pl.ds(chip * piece, piece)
        for which in range(2):
            all_ref[which, at_block(2 * chip + core, piece), :] = mine_ref[which, source, :]
            all_ref[which, at_block(2 * chip + 1 - core, piece), :] = cross_ref[which, source, :]


def chip_gradient_kernel(factor, lines, place_ref, prods_ref, cross_ref, far_ref, *refs):
    near_refs, pair_refs, refs = refs[:lines], refs[lines : 2 * lines], refs[2 * lines :]
    *out_refs, bands_ref, all_ref, grad_ref = refs
    chip, core, side, line = place_ref[0], place_ref[1], place_ref[2], place_ref[3]
    piece = near_refs[0].shape[0]
    interleave(all_ref, prods_ref, cross_ref, core, piece)
    for step in range(lines):
        near = at_block(2 * (line ^ step) + side, piece)
        far = at_block(2 * (line ^ step) + 1 - side, piece)
        bands_ref[0, near, :] = near_refs[step][...]
        bands_ref[0, far, :] = far_ref[pl.ds(step * piece, piece), :]
        bands_ref[1, near, :] = pair_refs[step][:piece, :]
        bands_ref[1, far, :] = pair_refs[step][piece:, :]
    total = jnp.dot(bands_ref[0], all_ref[1], preferred_element_type=jnp.float32)
    total += jnp.dot(bands_ref[1], all_ref[0], preferred_element_type=jnp.float32)
    grad_ref[...] = (factor * (4.0 * prods_ref[0].astype(jnp.float32) - 2.0 * total)).astype(jnp.bfloat16)
    for step, out_ref in enumerate(out_refs):
        out_ref[...] = grad_ref[at_block(chip ^ step, piece), :]


def finish_kernel(factor, piece, place_ref, mine_ref, cross_ref, trace_ref, out_ref, energy_ref, all_ref):
    bands = out_ref.shape[0]
    interleave(all_ref, mine_ref, cross_ref, place_ref[1], piece)
    ham, metric = all_ref[0], all_ref[1]
    out_ref[...] = factor * ham.astype(jnp.float32)
    row = lax.broadcasted_iota(jnp.int32, (bands, bands), 0)
    eye = row == lax.broadcasted_iota(jnp.int32, (bands, bands), 1)

    def diagonal(matrix):
        return jnp.sum(jnp.where(eye, matrix.astype(jnp.float32), 0.0), axis=0, keepdims=True)

    exact = trace_ref[...].astype(jnp.bfloat16).astype(jnp.float32)
    ham_exact, metric_exact = exact[0:1, :], exact[1:2, :]
    both = diagonal(jnp.dot(metric, ham, preferred_element_type=jnp.float32))
    both += metric_exact * ham_exact - diagonal(metric) * diagonal(ham)
    energy_ref[0, 0] = factor * jnp.sum(2.0 * ham_exact - both)


def by_chip(coeffs, ham_blocks, metric_blocks, block_cols, block_counts):
    devices = lax.axis_size("rows")
    index = lax.axis_index("rows")
    bands_dev, orbitals = coeffs.shape
    block_rows, slots, size, _ = ham_blocks.shape
    span = block_rows * size
    chips, lines, piece = devices // 2, devices // 4, bands_dev
    rows, bands, width = chips * piece, devices * piece, 2 * span
    chip = index // 2
    place = jnp.stack([chip, index % 2, chip % 2, chip // 2]).astype(jnp.int32)
    bf16, f32 = jnp.bfloat16, jnp.float32

    parts = whole_call(split_kernel, "split", (((piece, width), bf16),) * chips)(place, coeffs)
    cols = block_cols - chip * 2 * block_rows
    cols = jnp.where(cols < 0, cols + 3 * block_rows, cols)
    cols = jnp.where(jnp.arange(slots, dtype=jnp.int32)[None, :] < block_counts[:, None], cols, -1)
    got = [swap(parts[step], 2 * step) for step in range(chips - 1, 0, -1)][::-1]
    mine_in, mine_out, packed = expand_call(tie(cols, parts[0]), ham_blocks, metric_blocks)
    own, low, high = whole_call(
        stack_kernel, "stack", (((rows, width), bf16), ((rows, span), bf16), ((rows, span), bf16))
    )(place, tie(parts[0], mine_in), *got)
    left = lax.ppermute(high, "rows", [(i, i + 2) for i in range(devices - 2)])
    right = lax.ppermute(low, "rows", [(i + 2, i) for i in range(devices - 2)])
    other_in, other_out = expand_call(swap(cols, 1), swap(tie(packed, own), 1))

    every, sums = whole_call(
        functools.partial(inner_kernel, piece),
        "inner",
        (((bands, width), bf16), ((2, 2, rows, span), f32)),
        limit=32,
    )(place, own, swap(own, 1), mine_in, other_in)
    prods, keep_h, send_h, keep_m, *send_m, trace = whole_call(
        outer_kernel,
        "outer",
        (
            ((2, rows, width), bf16),
            ((lines, piece, bands), f32),
            ((lines, piece, bands), bf16),
            ((2 * piece, bands), f32),
        )
        + (((2 * piece, bands), bf16),) * (lines - 1)
        + (((8, bands), f32),),
        (pltpu.VMEM((2, rows, bands), f32),),
        limit=32,
    )(place, sums, every, left, right, mine_out, other_out)

    steps = range(1, lines)
    got_m = [swap(send, 4 * step) for step, send in zip(steps, send_m)]
    got_h = swap(send_h, 2)
    got_trace = swap(trace, 2)
    prods_cross = swap(prods, 1)
    keep_h, trace, *send_h = whole_call(
        sum_side_kernel,
        "sum_side",
        (((piece, bands), f32), ((8, bands), f32)) + (((piece, bands), bf16),) * (lines - 1),
    )(place, keep_h, got_h, trace, got_trace)
    got_h = [swap(send, 4 * step) for step, send in zip(steps, send_h)]
    keep_m, send_m = whole_call(
        sum_lines_kernel,
        "sum_lines",
        (((piece, bands), f32), ((piece, bands), bf16)),
        (pltpu.VMEM((2 * piece, bands), f32),),
    )(place, keep_m, *got_m)
    got_m = swap(send_m, 2)
    got_trace = swap(trace, 4)
    (metric,) = whole_call(last_metric_kernel, "last_metric", (((piece, bands), bf16),))(place, keep_m, got_m)
    ham, trace = whole_call(
        last_ham_kernel, "last_ham", (((piece, bands), bf16), ((8, bands), f32))
    )(place, keep_h, trace, got_trace, *got_h)
    near = [ham] + [swap(ham, 4 * step) for step in steps]
    pair = jnp.concatenate([metric, swap(metric, 2)])
    bit = 8
    while bit < devices:
        trace = trace + swap(trace, bit)
        bit *= 2
    trace = trace + swap(trace, 1)
    far = swap(jnp.concatenate(near), 2)
    pairs = [pair] + [swap(pair, 4 * step) for step in steps]

    factor = math.sqrt(orbitals)
    *grads, matrices = whole_call(
        functools.partial(chip_gradient_kernel, factor, lines),
        "chip_gradient",
        (((piece, width), bf16),) * chips + (((2, rows, bands), bf16),),
        (pltpu.VMEM((2, bands, width), bf16), pltpu.VMEM((rows, width), bf16)),
        limit=32,
    )(place, tie(prods, trace), prods_cross, far, *near, *pairs)
    grads = [grads[0]] + [swap(grad, 2 * step) for step, grad in enumerate(grads[1:], 1)]
    band_hamiltonian, energy = whole_call(
        functools.partial(finish_kernel, factor, piece),
        "finish",
        (((bands, bands), f32), ((1, 1), f32)),
        (pltpu.VMEM((2, bands, bands), bf16),),
        limit=32,
    )(place, matrices, swap(matrices, 1), trace)
    (gradient,) = whole_call(join_kernel, "join", (((piece, orbitals), bf16),))(
        place, tie(grads[0], energy), *grads[1:]
    )
    return (gradient, band_hamiltonian, energy.reshape(1))


def by_device(coeffs, ham_blocks, metric_blocks, block_cols, block_counts):
    devices = lax.axis_size("rows")
    index = lax.axis_index("rows")
    bands_dev, orbitals = coeffs.shape
    block_rows, _, size, _ = ham_blocks.shape
    span = block_rows * size
    bands = bands_dev * devices
    wide = expand(block_cols - (index - 1) * block_rows, block_counts, ham_blocks, metric_blocks)
    own = lax.all_to_all(
        coeffs.reshape(bands_dev, devices, span), "rows", split_axis=1, concat_axis=0, tiled=True
    ).reshape(bands, span)
    left = lax.ppermute(own, "rows", [(i, i + 1) for i in range(devices - 1)])
    right = lax.ppermute(own, "rows", [(i + 1, i) for i in range(devices - 1)])
    ham_prod, metric_prod, *grams = product(left, own, right, wide)
    ham_gram, metric_gram = lax.psum(grams, "rows")
    ham_band, metric_band = ham_gram.astype(jnp.bfloat16), metric_gram.astype(jnp.bfloat16)
    factor = math.sqrt(orbitals)
    grad_rows = gradient_of(factor, ham_band, metric_band, ham_prod, metric_prod)
    gradient = lax.all_to_all(
        grad_rows.reshape(devices, bands_dev, span), "rows", split_axis=0, concat_axis=2, tiled=True
    ).reshape(bands_dev, orbitals)
    ham_wide, metric_wide = ham_band.astype(jnp.float32), metric_band.astype(jnp.float32)
    energy = factor * (2.0 * jnp.trace(ham_wide) - jnp.sum(metric_wide * ham_wide.T))
    return (gradient, factor * ham_wide, energy.reshape(1))


def local(coeffs, *operators):
    devices, bands_dev = lax.axis_size("rows"), coeffs.shape[0]
    paired = devices >= 8 and devices & (devices - 1) == 0 and bands_dev % 16 == 0
    return (by_chip if paired else by_device)(coeffs, *operators)


def solution(mesh):
    in_specs = (
        P(("groups", "rows"), None),
        P(("groups", "rows"), None, None, None),
        P(("groups", "rows"), None, None, None),
        P(("groups", "rows"), None),
        P(("groups", "rows")),
    )
    out_specs = (P(("groups", "rows"), None), P("groups", None), P("groups"))
    return jax.shard_map(local, mesh=mesh, in_specs=in_specs, out_specs=out_specs, check_vma=False)
```

```python
import functools
import math

import jax
import jax.numpy as jnp
from jax import lax
from jax.experimental import pallas as pl
from jax.experimental.pallas import tpu as pltpu
from jax.sharding import PartitionSpec as P

NT = (((1,), (1,)), ((), ()))


def nt_dot(left, right):
    return lax.dot_general(left, right, NT, preferred_element_type=jnp.float32)


def expand_kernel(cols_ref, counts_ref, ham_ref, metric_ref, wide_ref, acc_ref):
    row = pl.program_id(0)
    slots, size = ham_ref.shape[1], ham_ref.shape[2]
    acc_ref[...] = jnp.zeros_like(acc_ref)
    half = lax.broadcasted_iota(jnp.int32, (size, 2 * size), 1) // size
    for slot in range(slots):
        col = cols_ref[row, slot]
        want = jnp.where(slot < counts_ref[row], col % 2, 2)
        keep = half == want
        lanes = pl.ds(pl.multiple_of((col // 2) * 2 * size, 2 * size), 2 * size)
        for which, blocks in enumerate((ham_ref, metric_ref)):
            block = blocks[0, slot].astype(jnp.float32)
            twice = jnp.concatenate([block, block], axis=1)
            acc_ref[which, :, lanes] += jnp.where(keep, twice, 0.0)
    wide_ref[...] = acc_ref[...].astype(wide_ref.dtype)


def expand(cols, counts, ham_blocks, metric_blocks):
    rows, slots, size, _ = ham_blocks.shape
    width = 3 * rows * size
    blocks_spec = pl.BlockSpec((1, slots, size, size), lambda b, *_: (b, 0, 0, 0))
    return pl.pallas_call(
        expand_kernel,
        out_shape=jax.ShapeDtypeStruct((2, rows * size, width), jnp.bfloat16),
        grid_spec=pltpu.PrefetchScalarGridSpec(
            num_scalar_prefetch=2,
            grid=(rows,),
            in_specs=[blocks_spec, blocks_spec],
            out_specs=pl.BlockSpec((2, size, width), lambda b, *_: (0, b, 0)),
            scratch_shapes=[pltpu.VMEM((2, size, width), jnp.float32)],
        ),
        compiler_params=pltpu.CompilerParams(vmem_limit_bytes=16 * 2**20),
        cost_estimate=pl.CostEstimate(
            flops=2 * ham_blocks.size, bytes_accessed=16 * 2**20, transcendentals=0
        ),
        name="expand",
    )(cols, counts, ham_blocks, metric_blocks)


def product_kernel(left_ref, own_ref, right_ref, all_ref, wide_ref, ham_ref, metric_ref, ham_gram_ref, metric_gram_ref):
    span = own_ref.shape[1]
    own = own_ref[...]

    def apply(which):
        total = nt_dot(own, wide_ref[which, :, span : 2 * span])
        total += nt_dot(left_ref[...], wide_ref[which, :, :span])
        return total + nt_dot(right_ref[...], wide_ref[which, :, 2 * span :])

    ham = apply(0).astype(jnp.bfloat16)
    metric = (own.astype(jnp.float32) + apply(1)).astype(jnp.bfloat16)
    ham_ref[...] = ham
    metric_ref[...] = metric
    ham_gram_ref[...] = nt_dot(ham, all_ref[...])
    metric_gram_ref[...] = nt_dot(metric, all_ref[...])


def product(left, own, right, wide, steps=2):
    bands, span = own.shape
    rows = bands // steps
    part = pl.BlockSpec((rows, span), lambda i, *_: (i, 0))
    square = pl.BlockSpec((rows, bands), lambda i, *_: (i, 0))
    return pl.pallas_call(
        product_kernel,
        out_shape=(
            jax.ShapeDtypeStruct((bands, span), jnp.bfloat16),
            jax.ShapeDtypeStruct((bands, span), jnp.bfloat16),
            jax.ShapeDtypeStruct((bands, bands), jnp.float32),
            jax.ShapeDtypeStruct((bands, bands), jnp.float32),
        ),
        grid_spec=pl.GridSpec(
            grid=(steps,),
            in_specs=[
                part,
                part,
                part,
                pl.BlockSpec((bands, span), lambda i, *_: (0, 0)),
                pl.BlockSpec(wide.shape, lambda i, *_: (0, 0, 0)),
            ],
            out_specs=[part, part, square, square],
        ),
        compiler_params=pltpu.CompilerParams(vmem_limit_bytes=32 * 2**20),
        cost_estimate=pl.CostEstimate(
            flops=2 * bands * span * (6 * span + 2 * bands), bytes_accessed=13 * 2**20, transcendentals=0
        ),
        name="product",
    )(left, own, right, own, wide)


def gradient_kernel(factor, ham_band_ref, metric_band_ref, part_ref, ham_ref, metric_ref, out_ref):
    total = jnp.dot(ham_band_ref[...], metric_ref[...], preferred_element_type=jnp.float32)
    total += jnp.dot(metric_band_ref[...], ham_ref[...], preferred_element_type=jnp.float32)
    out_ref[...] = (factor * (4.0 * part_ref[...].astype(jnp.float32) - 2.0 * total)).astype(jnp.bfloat16)


def gradient_of(factor, ham_band, metric_band, ham_prod, metric_prod, steps=2):
    bands, span = ham_prod.shape
    rows = bands // steps
    square = pl.BlockSpec((rows, bands), lambda i, *_: (i, 0))
    part = pl.BlockSpec((rows, span), lambda i, *_: (i, 0))
    whole = pl.BlockSpec((bands, span), lambda i, *_: (0, 0))
    return pl.pallas_call(
        functools.partial(gradient_kernel, factor),
        out_shape=jax.ShapeDtypeStruct((bands, span), jnp.bfloat16),
        grid_spec=pl.GridSpec(
            grid=(steps,),
            in_specs=[square, square, part, whole, whole],
            out_specs=part,
        ),
        compiler_params=pltpu.CompilerParams(vmem_limit_bytes=24 * 2**20),
        cost_estimate=pl.CostEstimate(
            flops=4 * bands * bands * span, bytes_accessed=6 * 2**20, transcendentals=0
        ),
        name="gradient",
    )(ham_band, metric_band, ham_prod, ham_prod, metric_prod)


def swap(value, bit):
    count = lax.axis_size("rows")
    return lax.ppermute(value, "rows", [(i, i ^ bit) for i in range(count)])


def fill_row(cols, blocks_of, acc_ref, size):
    half = lax.broadcasted_iota(jnp.int32, (size, 2 * size), 1) // size
    for slot, col in enumerate(cols):
        want = jnp.where(col < 0, 2, col % 2)
        lanes = at_block(jnp.maximum(col, 0) // 2, 2 * size)
        for which, block in enumerate(blocks_of(slot)):
            block = block.astype(jnp.float32)
            twice = jnp.concatenate([block, block], axis=1)
            acc_ref[which, :, lanes] += jnp.where(half == want, twice, 0.0)


def write_levels(acc_ref, inner_ref, outer_ref):
    total = acc_ref[...]
    high = total.astype(jnp.bfloat16)
    low = (total - high.astype(jnp.float32)).astype(jnp.bfloat16)
    width = inner_ref.shape[-1]
    for level, value in enumerate((high, low)):
        inner_ref[level] = value[:, :, :width]
        outer_ref[level] = value[:, :, width:]


def expand_own_kernel(cols_ref, ham_ref, metric_ref, inner_ref, outer_ref, packed_ref, acc_ref):
    row = pl.program_id(0)
    slots, size = ham_ref.shape[1], ham_ref.shape[2]
    acc_ref[...] = jnp.zeros_like(acc_ref)
    cols = [cols_ref[row, slot] for slot in range(slots)]
    fill_row(cols, lambda slot: (ham_ref[0, slot], metric_ref[0, slot]), acc_ref, size)
    write_levels(acc_ref, inner_ref, outer_ref)
    for which, blocks_ref in enumerate((ham_ref, metric_ref)):
        for slot in range(slots // 2):
            both = jnp.concatenate([blocks_ref[0, slot], blocks_ref[0, slot + slots // 2]], axis=1)
            packed_ref[which, 0, slot] = both


def expand_packed_kernel(cols_ref, packed_ref, inner_ref, outer_ref, acc_ref):
    row = pl.program_id(0)
    pairs, size = packed_ref.shape[2], packed_ref.shape[3]
    acc_ref[...] = jnp.zeros_like(acc_ref)

    def blocks_of(slot):
        lanes = slice(0, size) if slot < pairs else slice(size, 2 * size)
        return [packed_ref[which, 0, slot % pairs][:, lanes] for which in range(2)]

    fill_row([cols_ref[row, slot] for slot in range(2 * pairs)], blocks_of, acc_ref, size)
    write_levels(acc_ref, inner_ref, outer_ref)


def expand_call(cols, *blocks):
    rows, slots = cols.shape
    size = blocks[0].shape[3]
    span = rows * size
    packed = jax.ShapeDtypeStruct((2, rows, slots // 2, size, 2 * size), jnp.bfloat16)
    packed_spec = pl.BlockSpec((2, 1, slots // 2, size, 2 * size), lambda b, *_: (0, b, 0, 0, 0))
    blocks_spec = pl.BlockSpec((1, slots, size, size), lambda b, *_: (b, 0, 0, 0))
    own = len(blocks) == 2
    return pl.pallas_call(
        expand_own_kernel if own else expand_packed_kernel,
        out_shape=[
            jax.ShapeDtypeStruct((2, 2, span, 2 * span), jnp.bfloat16),
            jax.ShapeDtypeStruct((2, 2, span, span), jnp.bfloat16),
        ]
        + [packed] * own,
        grid_spec=pltpu.PrefetchScalarGridSpec(
            num_scalar_prefetch=1,
            grid=(rows,),
            in_specs=[blocks_spec, blocks_spec] if own else [packed_spec],
            out_specs=[
                pl.BlockSpec((2, 2, size, 2 * span), lambda b, *_: (0, 0, b, 0)),
                pl.BlockSpec((2, 2, size, span), lambda b, *_: (0, 0, b, 0)),
            ]
            + [packed_spec] * own,
            scratch_shapes=[pltpu.VMEM((2, size, 3 * span), jnp.float32)],
        ),
        compiler_params=pltpu.CompilerParams(vmem_limit_bytes=16 * 2**20),
        cost_estimate=pl.CostEstimate(flops=0, bytes_accessed=1024, transcendentals=0),
        name="expand_own" if own else "expand_packed",
    )(cols, *blocks)


def tie(value, *before):
    return lax.optimization_barrier((value, *before))[0]


def at_block(block, piece):
    return pl.ds(pl.multiple_of(block * piece, piece), piece)


def whole_call(kernel, name, outs, scratch=(), limit=8):
    vmem, smem = pl.BlockSpec(memory_space=pltpu.VMEM), pl.BlockSpec(memory_space=pltpu.SMEM)

    def call(scalars, *args):
        return pl.pallas_call(
            kernel,
            out_shape=tuple(jax.ShapeDtypeStruct(shape, dtype) for shape, dtype in outs),
            in_specs=[smem] + [vmem] * len(args),
            out_specs=tuple(smem if shape == (1, 1) else vmem for shape, _ in outs),
            scratch_shapes=scratch,
            compiler_params=pltpu.CompilerParams(vmem_limit_bytes=limit * 2**20),
            cost_estimate=pl.CostEstimate(flops=0, bytes_accessed=1024, transcendentals=0),
            name=name,
        )(scalars, *args)

    return call


def split_kernel(place_ref, coeffs_ref, *out_refs):
    width = out_refs[0].shape[1]
    for step, out_ref in enumerate(out_refs):
        out_ref[...] = coeffs_ref[:, at_block(place_ref[0] ^ step, width)]


def join_kernel(place_ref, *refs):
    *part_refs, out_ref = refs
    width = part_refs[0].shape[1]
    for step, part_ref in enumerate(part_refs):
        out_ref[:, at_block(place_ref[0] ^ step, width)] = part_ref[...]


def stack_kernel(place_ref, *refs):
    *part_refs, out_ref, low_ref, high_ref = refs
    piece, width = part_refs[0].shape
    for step, part_ref in enumerate(part_refs):
        rows = at_block(place_ref[0] ^ step, piece)
        part = part_ref[...]
        out_ref[rows, :] = part
        low_ref[rows, :] = part[:, : width // 2]
        high_ref[rows, :] = part[:, width // 2 :]


def inner_kernel(piece, place_ref, own_ref, cross_ref, mine_ref, other_ref, all_ref, sums_ref):
    core = place_ref[1]
    rows, width = own_ref.shape
    span = width // 2
    for chip in range(rows // piece):
        source = pl.ds(chip * piece, piece)
        all_ref[at_block(2 * chip + core, piece), :] = own_ref[source, :]
        all_ref[at_block(2 * chip + 1 - core, piece), :] = cross_ref[source, :]
    own = own_ref[...]
    for turn, wide_ref in enumerate((mine_ref, other_ref)):
        at = core if turn == 0 else 1 - core
        for which in range(2):
            total = nt_dot(own, wide_ref[1, which]) + nt_dot(own, wide_ref[0, which])
            if which == 1:
                total += own_ref[:, at_block(at, span)].astype(jnp.float32)
            sums_ref[turn, which] = total


def outer_kernel(
    place_ref, sums_ref, all_ref, left_ref, right_ref, mine_ref, other_ref,
    prods_ref, keep_h_ref, send_h_ref, keep_m_ref, *refs,
):
    *send_m_refs, trace_ref, gram_ref = refs
    core, side, line = place_ref[1], place_ref[2], place_ref[3]
    rows, span = left_ref.shape
    lines, piece = keep_h_ref.shape[:2]
    first = core == 0
    left, right = left_ref[...], right_ref[...]
    grams = [None, None]
    for turn, wide_ref in enumerate((mine_ref, other_ref)):
        at = core if turn == 0 else 1 - core
        outer = jnp.where(first, left, right) if turn == 0 else jnp.where(first, right, left)
        columns = at_block(at, span)
        for which in range(2):
            total = sums_ref[turn, which] + nt_dot(outer, wide_ref[1, which]) + nt_dot(outer, wide_ref[0, which])
            prod = total.astype(jnp.bfloat16)
            prods_ref[which, :, columns] = prod
            part = nt_dot(prod, all_ref[:, columns])
            grams[which] = part if grams[which] is None else grams[which] + part
    row = lax.broadcasted_iota(jnp.int32, (rows, 2 * rows), 0)
    col = lax.broadcasted_iota(jnp.int32, (rows, 2 * rows), 1)
    hit = col == row + (row // piece + core) * piece
    trace_ref[...] = jnp.zeros_like(trace_ref)
    for which in range(2):
        trace_ref[which : which + 1, :] = jnp.sum(jnp.where(hit, grams[which], 0.0), axis=0, keepdims=True)
        gram_ref[which] = grams[which]
    for at in range(lines):
        keep_h_ref[at] = gram_ref[0, at_block(2 * at + side, piece), :]
        send_h_ref[at] = gram_ref[0, at_block(2 * at + 1 - side, piece), :].astype(jnp.bfloat16)
    keep_m_ref[...] = gram_ref[1, at_block(line, 2 * piece), :]
    for step, send_ref in enumerate(send_m_refs, 1):
        send_ref[...] = gram_ref[1, at_block(line ^ step, 2 * piece), :].astype(jnp.bfloat16)


def sum_side_kernel(place_ref, keep_ref, got_ref, trace_ref, got_trace_ref, next_ref, next_trace_ref, *send_refs):
    line = place_ref[3]
    next_ref[...] = keep_ref[line] + got_ref[line].astype(jnp.float32)
    for step, send_ref in enumerate(send_refs, 1):
        at = line ^ step
        send_ref[...] = (keep_ref[at] + got_ref[at].astype(jnp.float32)).astype(jnp.bfloat16)
    next_trace_ref[...] = trace_ref[...] + got_trace_ref[...]


def sum_lines_kernel(place_ref, keep_ref, *refs):
    *got_refs, next_ref, send_ref, total_ref = refs
    side = place_ref[2]
    total = keep_ref[...]
    for got_ref in got_refs:
        total += got_ref[...].astype(jnp.float32)
    total_ref[...] = total
    piece = next_ref.shape[0]
    next_ref[...] = total_ref[at_block(side, piece), :]
    send_ref[...] = total_ref[at_block(1 - side, piece), :].astype(jnp.bfloat16)


def last_kernel(place_ref, keep_h_ref, keep_m_ref, got_m_ref, trace_ref, got_trace_ref, *refs):
    *got_refs, out_ref, next_trace_ref = refs
    total = keep_h_ref[...]
    for got_ref in got_refs:
        total += got_ref[...].astype(jnp.float32)
    out_ref[0] = total.astype(jnp.bfloat16)
    out_ref[1] = (keep_m_ref[...] + got_m_ref[...].astype(jnp.float32)).astype(jnp.bfloat16)
    next_trace_ref[...] = trace_ref[...] + got_trace_ref[...]


def interleave(all_ref, mine_ref, cross_ref, core, piece):
    for chip in range(mine_ref.shape[1] // piece):
        source = pl.ds(chip * piece, piece)
        for which in range(2):
            all_ref[which, at_block(2 * chip + core, piece), :] = mine_ref[which, source, :]
            all_ref[which, at_block(2 * chip + 1 - core, piece), :] = cross_ref[which, source, :]


def interleave_kernel(piece, place_ref, mine_ref, cross_ref, all_ref):
    interleave(all_ref, mine_ref, cross_ref, place_ref[1], piece)


def chip_gradient_kernel(factor, far, place_ref, prods_ref, all_ref, *refs):
    count = all_ref.shape[1] // (4 * refs[0].shape[1])
    piece_refs, refs = refs[:count], refs[count:]
    piece = piece_refs[0].shape[1]
    if far:
        near_refs, (*out_refs, bands_ref) = refs[:count], refs[count:]
    else:
        *out_refs, bands_ref = refs
    side, line = place_ref[2], place_ref[3]
    if far:
        side = 1 - side

    def rows_of(step, at):
        return at_block(2 * (line ^ step) + at, piece)

    if far:
        matrices_ref = out_refs.pop()
        for step in range(count):
            matrices_ref[:, rows_of(step, 1 - side), :] = near_refs[step][...]
            matrices_ref[:, rows_of(step, side), :] = piece_refs[step][...]
    for step in range(count):
        bands_ref[:, pl.ds(step * piece, piece), :] = piece_refs[step][...]
    total = jnp.dot(bands_ref[0], all_ref[1], preferred_element_type=jnp.float32)
    total += jnp.dot(bands_ref[1], all_ref[0], preferred_element_type=jnp.float32)
    for step, out_ref in enumerate(out_refs):
        part = 4.0 * prods_ref[0, rows_of(step, side), :].astype(jnp.float32)
        part -= 2.0 * total[step * piece : (step + 1) * piece, :]
        out_ref[...] = (factor * part).astype(jnp.bfloat16)


def finish_kernel(factor, piece, place_ref, mine_ref, cross_ref, trace_ref, out_ref, energy_ref, all_ref):
    bands = out_ref.shape[0]
    interleave(all_ref, mine_ref, cross_ref, place_ref[1], piece)
    ham, metric = all_ref[0], all_ref[1]
    out_ref[...] = factor * ham.astype(jnp.float32)
    row = lax.broadcasted_iota(jnp.int32, (bands, bands), 0)
    eye = row == lax.broadcasted_iota(jnp.int32, (bands, bands), 1)

    def diagonal(matrix):
        return jnp.sum(jnp.where(eye, matrix.astype(jnp.float32), 0.0), axis=0, keepdims=True)

    exact = trace_ref[...].astype(jnp.bfloat16).astype(jnp.float32)
    ham_exact, metric_exact = exact[0:1, :], exact[1:2, :]
    both = diagonal(jnp.dot(metric, ham, preferred_element_type=jnp.float32))
    both += metric_exact * ham_exact - diagonal(metric) * diagonal(ham)
    energy_ref[0, 0] = factor * jnp.sum(2.0 * ham_exact - both)


def by_chip(coeffs, ham_blocks, metric_blocks, block_cols, block_counts):
    devices = lax.axis_size("rows")
    index = lax.axis_index("rows")
    bands_dev, orbitals = coeffs.shape
    block_rows, slots, size, _ = ham_blocks.shape
    span = block_rows * size
    chips, lines, piece = devices // 2, devices // 4, bands_dev
    rows, bands, width = chips * piece, devices * piece, 2 * span
    chip = index // 2
    place = jnp.stack([chip, index % 2, chip % 2, chip // 2]).astype(jnp.int32)
    bf16, f32 = jnp.bfloat16, jnp.float32

    parts = whole_call(split_kernel, "split", (((piece, width), bf16),) * chips)(place, coeffs)
    cols = block_cols - chip * 2 * block_rows
    cols = jnp.where(cols < 0, cols + 3 * block_rows, cols)
    cols = jnp.where(jnp.arange(slots, dtype=jnp.int32)[None, :] < block_counts[:, None], cols, -1)
    got = [swap(parts[step], 2 * step) for step in range(chips - 1, 0, -1)][::-1]
    mine_in, mine_out, packed = expand_call(tie(cols, parts[0]), ham_blocks, metric_blocks)
    own, low, high = whole_call(
        stack_kernel, "stack", (((rows, width), bf16), ((rows, span), bf16), ((rows, span), bf16))
    )(place, tie(parts[0], mine_in), *got)
    left = lax.ppermute(high, "rows", [(i, i + 2) for i in range(devices - 2)])
    right = lax.ppermute(low, "rows", [(i + 2, i) for i in range(devices - 2)])
    other_in, other_out = expand_call(swap(cols, 1), swap(tie(packed, own), 1))

    every, sums = whole_call(
        functools.partial(inner_kernel, piece),
        "inner",
        (((bands, width), bf16), ((2, 2, rows, span), f32)),
        limit=32,
    )(place, own, swap(own, 1), mine_in, other_in)
    prods, keep_h, send_h, keep_m, *send_m, trace = whole_call(
        outer_kernel,
        "outer",
        (
            ((2, rows, width), bf16),
            ((lines, piece, bands), f32),
            ((lines, piece, bands), bf16),
            ((2 * piece, bands), f32),
        )
        + (((2 * piece, bands), bf16),) * (lines - 1)
        + (((8, bands), f32),),
        (pltpu.VMEM((2, rows, bands), f32),),
        limit=32,
    )(place, sums, every, left, right, mine_out, other_out)

    steps = range(1, lines)
    got_m = [swap(send, 4 * step) for step, send in zip(steps, send_m)]
    got_h = swap(send_h, 2)
    got_trace = swap(trace, 2)
    keep_h, trace, *send_h = whole_call(
        sum_side_kernel,
        "sum_side",
        (((piece, bands), f32), ((8, bands), f32)) + (((piece, bands), bf16),) * (lines - 1),
    )(place, keep_h, got_h, trace, got_trace)
    got_h = [swap(tie(send, *got_m), 4 * step) for step, send in zip(steps, send_h)]
    (prods_all,) = whole_call(
        functools.partial(interleave_kernel, piece), "interleave", (((2, bands, width), bf16),), limit=16
    )(place, prods, swap(prods, 1))
    keep_m, send_m = whole_call(
        sum_lines_kernel,
        "sum_lines",
        (((piece, bands), f32), ((piece, bands), bf16)),
        (pltpu.VMEM((2 * piece, bands), f32),),
    )(place, tie(keep_m, prods_all), *got_m)
    got_m = swap(send_m, 2)
    got_trace = swap(trace, 4)
    both = ((2, piece, bands), bf16)
    band, trace = whole_call(last_kernel, "last", (both, ((8, bands), f32)))(
        place, keep_h, keep_m, got_m, trace, got_trace, *got_h
    )
    near = [band] + [swap(band, 4 * step) for step in steps]
    far = [swap(part, 2) for part in near]
    bit = 8
    while bit < devices:
        trace = trace + swap(trace, bit)
        bit *= 2

    total_trace = trace + swap(trace, 1)
    factor = math.sqrt(orbitals)
    part = ((piece, width), bf16)
    bands_half = pltpu.VMEM((2, rows // 2, bands), bf16)
    grads = whole_call(
        functools.partial(chip_gradient_kernel, factor, False), "gradient_near", (part,) * lines, (bands_half,), limit=32
    )(place, tie(prods, far[0], far[1], trace), prods_all, *near)
    got_near = [grads[0]] + [swap(grads[step], 4 * step) for step in steps]
    *grads, matrices = whole_call(
        functools.partial(chip_gradient_kernel, factor, True),
        "gradient_far",
        (part,) * lines + (((2, rows, bands), bf16),),
        (bands_half,),
        limit=32,
    )(place, tie(prods, total_trace, *got_near), prods_all, *far, *near)
    got_far = [swap(grad, 4 * step + 2) for step, grad in enumerate(grads)]
    grads = [value for pair in zip(got_near, got_far) for value in pair]
    band_hamiltonian, energy = whole_call(
        functools.partial(finish_kernel, factor, piece),
        "finish",
        (((bands, bands), f32), ((1, 1), f32)),
        (pltpu.VMEM((2, bands, bands), bf16),),
        limit=32,
    )(place, matrices, swap(matrices, 1), total_trace)
    (gradient,) = whole_call(join_kernel, "join", (((piece, orbitals), bf16),))(
        place, tie(grads[0], energy), *grads[1:]
    )
    return (gradient, band_hamiltonian, energy.reshape(1))


def by_device(coeffs, ham_blocks, metric_blocks, block_cols, block_counts):
    devices = lax.axis_size("rows")
    index = lax.axis_index("rows")
    bands_dev, orbitals = coeffs.shape
    block_rows, _, size, _ = ham_blocks.shape
    span = block_rows * size
    bands = bands_dev * devices
    wide = expand(block_cols - (index - 1) * block_rows, block_counts, ham_blocks, metric_blocks)
    own = lax.all_to_all(
        coeffs.reshape(bands_dev, devices, span), "rows", split_axis=1, concat_axis=0, tiled=True
    ).reshape(bands, span)
    left = lax.ppermute(own, "rows", [(i, i + 1) for i in range(devices - 1)])
    right = lax.ppermute(own, "rows", [(i + 1, i) for i in range(devices - 1)])
    ham_prod, metric_prod, *grams = product(left, own, right, wide)
    ham_gram, metric_gram = lax.psum(grams, "rows")
    ham_band, metric_band = ham_gram.astype(jnp.bfloat16), metric_gram.astype(jnp.bfloat16)
    factor = math.sqrt(orbitals)
    grad_rows = gradient_of(factor, ham_band, metric_band, ham_prod, metric_prod)
    gradient = lax.all_to_all(
        grad_rows.reshape(devices, bands_dev, span), "rows", split_axis=0, concat_axis=2, tiled=True
    ).reshape(bands_dev, orbitals)
    ham_wide, metric_wide = ham_band.astype(jnp.float32), metric_band.astype(jnp.float32)
    energy = factor * (2.0 * jnp.trace(ham_wide) - jnp.sum(metric_wide * ham_wide.T))
    return (gradient, factor * ham_wide, energy.reshape(1))


def local(coeffs, *operators):
    devices, bands_dev = lax.axis_size("rows"), coeffs.shape[0]
    paired = devices >= 8 and devices & (devices - 1) == 0 and bands_dev % 16 == 0
    return (by_chip if paired else by_device)(coeffs, *operators)


def solution(mesh):
    in_specs = (
        P(("groups", "rows"), None),
        P(("groups", "rows"), None, None, None),
        P(("groups", "rows"), None, None, None),
        P(("groups", "rows"), None),
        P(("groups", "rows")),
    )
    out_specs = (P(("groups", "rows"), None), P("groups", None), P("groups"))
    return jax.shard_map(local, mesh=mesh, in_specs=in_specs, out_specs=out_specs, check_vma=False)
```
